256 devices in a mesh: pix: 64 (over z, y, core), band: 4 (over x).
Axes of the slice: x: 4, y: 4, z: 8, core: 2. Of those that a mesh axis runs over, the one named last changes fastest.
Arguments:
- series: bfloat16 [224, 128, 16384], P('band', None, 'pix'), may hold values from 0 to 1
- pixel_factor: float32 [64, 16384], P(None, 'pix'), may hold values from 0.03 to 0.6
- band_factor: float32 [224, 64], P('band'), may hold values from 0.03 to 0.6
- time_factor: float32 [128, 64], replicated, may hold values from 0.03 to 0.6
Outputs:
- pixels_out: float32 [64, 16384], P(None, 'pix')
- bands_out: float32 [224, 64], P('band')
- times_out: float32 [128, 64], replicated
The draws below stay inside these ranges and needn't reach their ends.
All inputs are finite; a program needn't handle non-finite values.
Results may differ from the reference program's by a relative error of at most 0.00045.
Values sent between devices are 32-bit elements; how exact they have to be, the bound alone decides.
A program may use at most 64 MiB of HBM per device.

```python
import math
import jax
import jax.numpy as jnp
from jax import lax

RANK = 64
BANDS = 224
TIMES = 128
PIX_DEV = 256
SWEEPS = 4
PIX = 16384


def level_of(stream_key, dims, cuts, least, high):
    factor_of, own = 1.0, jax.random.fold_in(stream_key, 6)
    for position, parts in cuts:
        draws = jnp.exp(jax.random.uniform(jax.random.fold_in(own, position), (parts,), jnp.float32, least / len(cuts), high / len(cuts)))
        factor_of = factor_of * jnp.repeat(draws, dims[position] // parts).reshape([-1 if axis == position else 1 for axis in range(len(dims))])
    return factor_of


def setup_inputs(seed: int = 0) -> dict:
    arg_keys = jax.random.split(jax.random.key(seed), 5)
    series = jnp.clip(1.0 * jax.random.uniform(arg_keys[0], (BANDS, TIMES, PIX), jnp.float32) ** level_of(arg_keys[0], (BANDS, TIMES, PIX), ((0, 4), (2, 64)), -0.2, 0.2), 0.0, 1.0).astype(jnp.bfloat16)
    pixel_factor = jnp.clip(jnp.exp(math.log(0.6) - 2.9957323 * jax.random.uniform(arg_keys[1], (RANK, PIX), jnp.float32) ** level_of(arg_keys[1], (RANK, PIX), ((1, 64),), -0.2, 0.2)), 0.03, 0.6)
    band_factor = jnp.clip(jnp.exp(math.log(0.6) - 2.9957323 * jax.random.uniform(arg_keys[2], (BANDS, RANK), jnp.float32) ** level_of(arg_keys[2], (BANDS, RANK), ((0, 4),), -0.2, 0.2)), 0.03, 0.6)
    time_factor = jnp.clip(jnp.exp(jax.random.uniform(arg_keys[3], (TIMES, RANK), jnp.float32, math.log(0.03), math.log(0.6))), 0.03, 0.6)
    return dict(series=series, pixel_factor=pixel_factor, band_factor=band_factor, time_factor=time_factor)


HIGH = lax.Precision.HIGHEST


def step_of(gram):
    return 1.0 / (jnp.max(jnp.sum(gram, axis=1)) + 1e-6)


def reference(series, pixel_factor, band_factor, time_factor):
    width = PIX_DEV
    count = PIX // width
    pixels = pixel_factor
    bands = band_factor
    times = time_factor
    gram_b = jnp.dot(bands.T, bands, precision=HIGH, preferred_element_type=jnp.float32)
    for sweep in range(SWEEPS):
        gram_c = jnp.dot(times.T, times, precision=HIGH, preferred_element_type=jnp.float32)
        c_low = times.astype(jnp.bfloat16).astype(jnp.float32)
        gram = gram_b * gram_c
        scale = step_of(gram)

        def first_pass(carry, index):
            gram_acc, target_acc = carry
            start = (index * width).astype(jnp.int32)
            block = lax.dynamic_slice_in_dim(series, start, width, 2).astype(jnp.float32)
            old = lax.dynamic_slice_in_dim(pixels, start, width, 1)
            folded = jnp.einsum("btp,tr->brp", block, c_low, precision=HIGH)
            target = jnp.einsum("brp,br->rp", folded, bands, precision=HIGH)
            fresh = jnp.maximum(old - scale * (jnp.dot(gram, old, precision=HIGH) - target), 0.0)
            gram_acc = gram_acc + jnp.dot(fresh, fresh.T, precision=HIGH)
            target_acc = target_acc + jnp.einsum("brp,rp->br", folded, fresh, precision=HIGH)
            return (gram_acc, target_acc), fresh

        start_carry = (jnp.zeros((RANK, RANK), jnp.float32), jnp.zeros((BANDS, RANK), jnp.float32))
        (gram_a, target_b), blocks = lax.scan(first_pass, start_carry, jnp.arange(count, dtype=jnp.int32))
        pixels = jnp.transpose(blocks, (1, 0, 2)).reshape(RANK, PIX)
        gram = gram_a * gram_c
        bands = jnp.maximum(bands - step_of(gram) * (jnp.dot(bands, gram, precision=HIGH) - target_b), 0.0)
        gram_b = jnp.dot(bands.T, bands, precision=HIGH, preferred_element_type=jnp.float32)
        p_low = pixels.astype(jnp.bfloat16).astype(jnp.float32)
        b_low = bands.astype(jnp.bfloat16).astype(jnp.float32)

        def second_pass(carry, index):
            start = (index * width).astype(jnp.int32)
            block = lax.dynamic_slice_in_dim(series, start, width, 2).astype(jnp.float32)
            low = lax.dynamic_slice_in_dim(p_low, start, width, 1)
            return carry + jnp.einsum("btp,rp->brt", block, low, precision=HIGH), None

        spread, unused = lax.scan(second_pass, jnp.zeros((BANDS, RANK, TIMES), jnp.float32), jnp.arange(count, dtype=jnp.int32))
        target_c = jnp.einsum("brt,br->tr", spread, b_low, precision=HIGH)
        gram = gram_a * gram_b
        times = jnp.maximum(times - step_of(gram) * (jnp.dot(times, gram, precision=HIGH) - target_c), 0.0)
    return pixels, bands, times
```

```python
import functools

import jax
import jax.numpy as jnp
from jax import lax
from jax.experimental import pallas as pl
from jax.experimental.pallas import tpu as pltpu
from jax.sharding import PartitionSpec as P

SWEEPS = 4
RANK = 64
LANES = 128
UNROLL = 8
F32 = jnp.float32
HIGH = lax.Precision.HIGHEST
MESH = pl.DeviceIdType.MESH

AT_PIXELS, AT_GRAM, B_SCATTER, B_Z, B_GATHER, C_SCATTER, C_Z, C_X, C_GATHER = range(9)


def dot_nn(a, b):
    return lax.dot_general(
        a, b, (((1,), (0,)), ((), ())), precision=HIGH, preferred_element_type=F32
    )


def dot_nt(a, b):
    return lax.dot_general(
        a, b, (((1,), (1,)), ((), ())), precision=HIGH, preferred_element_type=F32
    )


def padded_gram(a):
    return dot_nt(a, jnp.concatenate([a, jnp.zeros_like(a)], axis=0))


def step_of(gram):
    sums = jnp.sum(gram, axis=0, keepdims=True)
    return 1.0 / (jnp.max(sums, axis=1, keepdims=True) + 1e-06)


def total_of(slots):
    total = slots[0]
    for j in range(1, slots.shape[0]):
        total = total + slots[j]
    return total


def kernel(
    nx, nz, inner,
    series, pixels_in, bands_in, times_in,
    pixels, bands, times,
    gram_b, wide, folded, spread,
    a_slots, g_slots,
    b_send, b_parts, b_z, b_all,
    c_send, c_parts, c_z, c_x, c_all,
    send_sems, recv_sems,
):
    nb = series.shape[0]
    pix_me = lax.axis_index("pix")
    x_me = lax.axis_index("band")
    z_me = pix_me // inner
    i_me = lax.rem(pix_me, inner)

    def on_x(k):
        return (pix_me, k)

    def on_z(k):
        return (k * inner + i_me, x_me)

    def on_inner(k):
        return (z_me * inner + k, x_me)

    groups = ((on_x, x_me, nx), (on_z, z_me, nz), (on_inner, i_me, inner))
    barrier = pltpu.get_barrier_semaphore()
    for at, me, n in groups:
        for d in range(1, n):
            pl.semaphore_signal(
                barrier, inc=1, device_id=at(lax.rem(me + d, n)), device_id_type=MESH
            )
    pl.semaphore_wait(barrier, sum(n - 1 for _, _, n in groups))

    def copies_of(phase, group, source, slots, sent):
        at, me, n = group
        copies = []
        for d in range(1, n):
            to = lax.rem(me + d, n)
            slot = me if sent else lax.rem(me + n - d, n)
            copies.append(
                pltpu.make_async_remote_copy(
                    src_ref=slots.at[me] if source is None else source.at[to],
                    dst_ref=slots.at[slot],
                    send_sem=send_sems.at[phase, d],
                    recv_sem=recv_sems.at[phase, d],
                    device_id=at(to),
                    device_id_type=MESH,
                )
            )
        return copies

    def start(phase, group, source, slots):
        for copy in copies_of(phase, group, source, slots, True):
            copy.start()

    def finish(phase, group, source, slots):
        for copy in copies_of(phase, group, source, slots, False):
            copy.wait_recv()
        for copy in copies_of(phase, group, source, slots, True):
            copy.wait_send()

    x_group, z_group, in_group = groups
    lane = lax.broadcasted_iota(jnp.int32, (RANK, LANES), 1)

    def column(value, b):
        return jnp.broadcast_to(value[:, RANK + b : RANK + b + 1], (RANK, LANES))

    pixels[...] = pixels_in[...]
    times[...] = times_in[...]
    first = bands_in[...]
    bands[...] = first
    g_slots[x_me] = padded_gram(first)
    start(AT_GRAM, x_group, None, g_slots)
    for b in range(nb):
        wide[b] = column(first, b)
    finish(AT_GRAM, x_group, None, g_slots)
    gram_b[...] = total_of(g_slots)

    def sweep(_, carry):
        ct = times[...]
        gram_c = dot_nt(ct, ct)
        c_low = ct.astype(jnp.bfloat16)

        def fold(i, acc):
            for u in range(UNROLL):
                b = i * UNROLL + u
                one = jnp.dot(c_low, series[b], preferred_element_type=F32)
                folded[b] = one
                weight = wide[b]
                acc = acc + one * jnp.concatenate([weight, weight], axis=1)
            return acc

        a_slots[x_me] = lax.fori_loop(
            0, nb // UNROLL, fold, jnp.zeros(pixels.shape, F32)
        )
        start(AT_PIXELS, x_group, None, a_slots)
        gram = gram_b[...][:, :RANK] * gram_c
        scale = step_of(gram)
        p = pixels[...]
        moved = dot_nn(gram, p)
        finish(AT_PIXELS, x_group, None, a_slots)
        p = jnp.maximum(p - scale * (moved - total_of(a_slots)), 0.0)
        pixels[...] = p
        p_low = p.astype(jnp.bfloat16)

        def into_bands(i, acc):
            for u in range(UNROLL):
                b = i * UNROLL + u
                both = folded[b] * p
                half = both[:, :LANES] + both[:, LANES:]
                acc = jnp.where(
                    lane == RANK + b, jnp.sum(half, axis=1, keepdims=True), acc
                )
            return acc

        both = lax.fori_loop(0, nb // UNROLL, into_bands, padded_gram(p))
        b_send[...] = both.reshape(b_send.shape)
        b_parts[i_me] = b_send[i_me]

        def spread_over(low, high):
            def some(i, carry):
                for u in range(UNROLL):
                    b = i * UNROLL + u
                    spread[b] = lax.dot_general(
                        p_low, series[b], (((1,), (1,)), ((), ())),
                        preferred_element_type=F32,
                    )
                return carry

            lax.fori_loop(low, high, some, 0)

        blocks = nb // UNROLL
        cuts = (0, (blocks * 3 + 6) // 7, (blocks * 5 + 6) // 7, blocks)
        start(B_SCATTER, in_group, b_send, b_parts)
        spread_over(cuts[0], cuts[1])
        finish(B_SCATTER, in_group, b_send, b_parts)
        b_z[z_me] = total_of(b_parts)
        start(B_Z, z_group, None, b_z)
        spread_over(cuts[1], cuts[2])
        finish(B_Z, z_group, None, b_z)
        b_all[i_me] = total_of(b_z)
        start(B_GATHER, in_group, None, b_all)
        spread_over(cuts[2], cuts[3])
        finish(B_GATHER, in_group, None, b_all)
        both = b_all[...].reshape(RANK, LANES)
        gram_a = both[:, :RANK]
        target = jnp.where(lane >= RANK, both, 0.0)
        gram = gram_a * gram_c
        bt = bands[...]
        bt = jnp.maximum(bt - step_of(gram) * (dot_nn(gram, bt) - target), 0.0)
        bands[...] = bt
        g_slots[x_me] = padded_gram(bt)
        start(AT_GRAM, x_group, None, g_slots)

        acc = jnp.zeros((RANK, LANES), F32)
        for b in range(nb):
            weight = column(bt, b)
            wide[b] = weight
            acc = acc + spread[b] * weight.astype(jnp.bfloat16).astype(F32)
        c_send[...] = acc.reshape(c_send.shape)
        c_parts[i_me] = c_send[i_me]
        start(C_SCATTER, in_group, c_send, c_parts)
        finish(C_SCATTER, in_group, c_send, c_parts)
        c_z[z_me] = total_of(c_parts)
        start(C_Z, z_group, None, c_z)
        finish(AT_GRAM, x_group, None, g_slots)
        new_gram = total_of(g_slots)
        gram_b[...] = new_gram
        gram = gram_a * new_gram[:, :RANK]
        scale = step_of(gram)
        moved = dot_nn(gram, ct)
        finish(C_Z, z_group, None, c_z)
        c_x[x_me] = total_of(c_z)
        start(C_X, x_group, None, c_x)
        finish(C_X, x_group, None, c_x)
        c_all[i_me] = total_of(c_x)
        start(C_GATHER, in_group, None, c_all)
        finish(C_GATHER, in_group, None, c_all)
        target = c_all[...].reshape(RANK, LANES)
        times[...] = jnp.maximum(ct - scale * (moved - target), 0.0)
        return carry

    lax.fori_loop(0, SWEEPS, sweep, 0)


def body(nx, nz, inner, series, pixel_factor, band_factor, time_factor):
    nb = series.shape[0]
    rows = RANK // inner
    bands_in = jnp.pad(band_factor.T, ((0, 0), (RANK, LANES - RANK - nb)))
    vmem = pl.BlockSpec(memory_space=pltpu.VMEM)
    wide = (RANK, LANES)
    pixels, bands, times = pl.pallas_call(
        functools.partial(kernel, nx, nz, inner),
        out_shape=(
            jax.ShapeDtypeStruct(pixel_factor.shape, F32),
            jax.ShapeDtypeStruct(wide, F32),
            jax.ShapeDtypeStruct(wide, F32),
        ),
        in_specs=[vmem] * 4,
        out_specs=(vmem,) * 3,
        scratch_shapes=[
            pltpu.VMEM(wide, F32),
            pltpu.VMEM((nb,) + wide, F32),
            pltpu.VMEM((nb,) + pixel_factor.shape, F32),
            pltpu.VMEM((nb,) + wide, F32),
            pltpu.VMEM((nx,) + pixel_factor.shape, F32),
            pltpu.VMEM((nx,) + wide, F32),
            pltpu.VMEM((inner, rows, LANES), F32),
            pltpu.VMEM((inner, rows, LANES), F32),
            pltpu.VMEM((nz, rows, LANES), F32),
            pltpu.VMEM((inner, rows, LANES), F32),
            pltpu.VMEM((inner, rows, LANES), F32),
            pltpu.VMEM((inner, rows, LANES), F32),
            pltpu.VMEM((nz, rows, LANES), F32),
            pltpu.VMEM((nx, rows, LANES), F32),
            pltpu.VMEM((inner, rows, LANES), F32),
            pltpu.SemaphoreType.DMA((9, 8)),
            pltpu.SemaphoreType.DMA((9, 8)),
        ],
        compiler_params=pltpu.CompilerParams(collective_id=0, has_side_effects=True),
    )(series, pixel_factor, bands_in, time_factor.T)
    return pixels, bands[:, RANK : RANK + nb].T, times.T


def build(mesh, inner):
    placed = (P("band", None, "pix"), P(None, "pix"), P("band", None), P())
    return jax.shard_map(
        functools.partial(body, mesh.shape["band"], mesh.shape["pix"] // inner, inner),
        mesh=mesh,
        in_specs=placed,
        out_specs=(P(None, "pix"), P("band", None), P()),
        check_vma=False,
    )


def solution(mesh):
    return build(mesh, 8)
```

```python
import functools

import jax
import jax.numpy as jnp
from jax import lax
from jax.experimental import pallas as pl
from jax.experimental.pallas import tpu as pltpu
from jax.sharding import PartitionSpec as P

SWEEPS = 4
RANK = 64
LANES = 128
UNROLL = 8
F32 = jnp.float32
HIGH = lax.Precision.HIGHEST
MESH = pl.DeviceIdType.MESH

(
    AT_PIXELS, AT_GRAM, AT_FIRST, B_PAIR, B_Y, B_Z, B_BACK,
    C_PAIR, C_Y, C_X, C_Z, C_BACK, PHASES,
) = range(13)
HALF = RANK // 2


def dot_nn(a, b):
    return lax.dot_general(
        a, b, (((1,), (0,)), ((), ())), precision=HIGH, preferred_element_type=F32
    )


def dot_nt(a, b):
    return lax.dot_general(
        a, b, (((1,), (1,)), ((), ())), precision=HIGH, preferred_element_type=F32
    )


def padded_gram(a):
    return dot_nt(a, jnp.concatenate([a, jnp.zeros_like(a)], axis=0))


def step_of(gram):
    sums = jnp.sum(gram, axis=0, keepdims=True)
    return 1.0 / (jnp.max(sums, axis=1, keepdims=True) + 1e-06)


def total_of(slots):
    total = slots[0]
    for j in range(1, slots.shape[0]):
        total = total + slots[j]
    return total


def kernel(
    nx, ny, nz,
    series_in, pixels_in, bands_in, times_in,
    pixels, bands_out, times,
    series, bands, gram_b, wide, folded, spread,
    a_slots, g_slots, first_slots,
    b_send, b_pair, b_y, b_z, b_all,
    c_send, c_pair, c_y, c_x, c_z, c_all,
    send_sems, recv_sems, load_sem,
):
    nb = series.shape[0]
    load = pltpu.make_async_copy(series_in, series, load_sem)
    load.start()
    pix_me = lax.axis_index("pix")
    x_me = lax.axis_index("band")
    z_me = pix_me // (2 * ny)
    y_me = lax.rem(pix_me // 2, ny)
    c_me = lax.rem(pix_me, 2)

    def on_x(k):
        return (pix_me, k)

    def on_z(k):
        return (k * (2 * ny) + y_me * 2 + c_me, x_me)

    def on_y(k):
        return (z_me * (2 * ny) + k * 2 + c_me, x_me)

    def on_core(k):
        return (z_me * (2 * ny) + y_me * 2 + k, x_me)

    groups = ((on_x, x_me, nx), (on_z, z_me, nz), (on_y, y_me, ny), (on_core, c_me, 2))
    x_group, z_group, y_group, core_group = groups
    barrier = pltpu.get_barrier_semaphore()
    for at, me, n in groups:
        for d in range(1, n):
            pl.semaphore_signal(
                barrier, inc=1, device_id=at(lax.rem(me + d, n)), device_id_type=MESH
            )
    pl.semaphore_wait(barrier, sum(n - 1 for _, _, n in groups))

    def copies_of(phase, group, source, slots, sent):
        at, me, n = group
        copies = []
        for d in sorted(range(1, n), key=lambda d: -min(d, n - d)):
            to = lax.rem(me + d, n)
            slot = me if sent else lax.rem(me + n - d, n)
            copies.append(
                pltpu.make_async_remote_copy(
                    src_ref=slots.at[me] if source is None else source,
                    dst_ref=slots if source is not None else slots.at[slot],
                    send_sem=send_sems.at[phase, d],
                    recv_sem=recv_sems.at[phase, d],
                    device_id=at(to),
                    device_id_type=MESH,
                )
            )
        return copies

    def start(phase, group, slots, source=None):
        for copy in copies_of(phase, group, source, slots, True):
            copy.start()

    def arrived(phase, group, slots, source=None):
        for copy in copies_of(phase, group, source, slots, False):
            copy.wait_recv()

    def sent(phase, group, slots, source=None):
        for copy in copies_of(phase, group, source, slots, True):
            copy.wait_send()

    lane = lax.broadcasted_iota(jnp.int32, (RANK, LANES), 1)
    half_lane = lax.broadcasted_iota(jnp.int32, (HALF, LANES), 1)
    mine = pl.multiple_of(c_me * HALF, HALF)
    other = pl.multiple_of((1 - c_me) * HALF, HALF)

    def column(value, b):
        one = value[:, RANK + b : RANK + b + 1]
        return jnp.broadcast_to(one, (value.shape[0], LANES))

    rest = LANES - RANK - nb
    tall = [jnp.zeros((RANK, RANK), F32), bands_in[...]]
    if rest:
        tall.append(jnp.zeros((rest, RANK), F32))
    unit = (
        lax.broadcasted_iota(jnp.int32, (RANK, RANK), 0)
        == lax.broadcasted_iota(jnp.int32, (RANK, RANK), 1)
    ).astype(F32)
    first = dot_nt(unit, jnp.concatenate(tall, axis=0))
    bands[...] = first
    first_slots[x_me] = padded_gram(first)
    start(AT_FIRST, x_group, first_slots)
    pixels[...] = pixels_in[...]
    times[...] = times_in[...]
    for b in range(nb):
        wide[b] = column(first, b)
    load.wait()

    def sweep(number, carry):
        ct = times[...]
        c_low = ct.astype(jnp.bfloat16)

        def fold(i, acc):
            for u in range(UNROLL):
                b = i * UNROLL + u
                one = jnp.dot(c_low, series[b], preferred_element_type=F32)
                folded[b] = one
                weight = wide[b]
                acc = acc + one * jnp.concatenate([weight, weight], axis=1)
            return acc

        acc = lax.fori_loop(0, nb // UNROLL, fold, jnp.zeros(pixels.shape, F32))
        a_slots[x_me] = acc
        start(AT_PIXELS, x_group, a_slots)

        @pl.when(number == 0)
        def _():
            arrived(AT_FIRST, x_group, first_slots)
            sent(AT_FIRST, x_group, first_slots)
            gram_b[...] = total_of(first_slots)

        gram_c = dot_nt(ct, ct)
        gram = gram_b[...][:, :RANK] * gram_c
        scale = step_of(gram)
        p = pixels[...]
        moved = p - scale * dot_nn(gram, p)
        arrived(AT_PIXELS, x_group, a_slots)
        p = jnp.maximum(moved + scale * total_of(a_slots), 0.0)
        pixels[...] = p
        p_low = p.astype(jnp.bfloat16)
        p_tall = jnp.concatenate([p, jnp.zeros_like(p)], axis=0)

        def band_part(low):
            rows = pl.ds(low, HALF)
            p_rows = pixels[rows, :]

            def into_bands(i, acc):
                for u in range(UNROLL):
                    b = i * UNROLL + u
                    both = folded[b, rows, :] * p_rows
                    both = both[:, :LANES] + both[:, LANES:]
                    acc = jnp.where(
                        half_lane == RANK + b,
                        jnp.sum(both, axis=1, keepdims=True), acc,
                    )
                return acc

            return lax.fori_loop(0, nb // UNROLL, into_bands, dot_nt(p_rows, p_tall))

        def spread_over(low, high):
            def some(i, carry):
                for u in range(UNROLL):
                    b = i * UNROLL + u
                    spread[b] = lax.dot_general(
                        p_low, series[b], (((1,), (1,)), ((), ())),
                        preferred_element_type=F32,
                    )
                return carry

            lax.fori_loop(low, high, some, 0)

        blocks = nb // UNROLL
        cuts = (0, (blocks + 6) // 7, (blocks * 4 + 6) // 7, blocks)
        b_send[...] = band_part(other)
        start(B_PAIR, core_group, b_pair, b_send)
        own = band_part(mine)
        sent(AT_PIXELS, x_group, a_slots)
        spread_over(cuts[0], cuts[1])
        arrived(B_PAIR, core_group, b_pair, b_send)
        b_y[y_me] = own + b_pair[...]
        start(B_Y, y_group, b_y)
        sent(B_PAIR, core_group, b_pair, b_send)
        spread_over(cuts[1], cuts[2])
        arrived(B_Y, y_group, b_y)
        b_z[z_me] = total_of(b_y)
        start(B_Z, z_group, b_z)
        sent(B_Y, y_group, b_y)
        spread_over(cuts[2], cuts[3])
        arrived(B_Z, z_group, b_z)
        b_all[c_me] = total_of(b_z)
        start(B_BACK, core_group, b_all)
        sent(B_Z, z_group, b_z)
        arrived(B_BACK, core_group, b_all)
        both = b_all[...].reshape(RANK, LANES)
        gram_a = both[:, :RANK]
        target = jnp.where(lane >= RANK, both, 0.0)
        gram = gram_a * gram_c
        bt = bands[...]
        bt = jnp.maximum(bt - step_of(gram) * (dot_nn(gram, bt) - target), 0.0)
        bands[...] = bt

        def time_part(low):
            rows = pl.ds(low, HALF)
            bt_rows = bands[rows, :]
            acc = jnp.zeros((HALF, LANES), F32)
            for b in range(nb):
                weight = column(bt_rows, b)
                wide[b, rows, :] = weight
                weight = weight.astype(jnp.bfloat16).astype(F32)
                acc = acc + spread[b, rows, :] * weight
            return acc

        c_send[...] = time_part(other)
        start(C_PAIR, core_group, c_pair, c_send)
        sent(B_BACK, core_group, b_all)
        g_slots[x_me] = padded_gram(bt)
        start(AT_GRAM, x_group, g_slots)
        own = time_part(mine)
        arrived(C_PAIR, core_group, c_pair, c_send)
        c_y[y_me] = own + c_pair[...]
        start(C_Y, y_group, c_y)
        sent(C_PAIR, core_group, c_pair, c_send)
        arrived(C_Y, y_group, c_y)
        c_x[x_me] = total_of(c_y)
        start(C_X, x_group, c_x)
        sent(C_Y, y_group, c_y)
        arrived(C_X, x_group, c_x)
        c_z[z_me] = total_of(c_x)
        start(C_Z, z_group, c_z)
        sent(C_X, x_group, c_x)
        arrived(AT_GRAM, x_group, g_slots)
        sent(AT_GRAM, x_group, g_slots)
        new_gram = total_of(g_slots)
        gram_b[...] = new_gram
        gram = gram_a * new_gram[:, :RANK]
        scale = step_of(gram)
        moved = ct - scale * dot_nn(gram, ct)
        arrived(C_Z, z_group, c_z)
        c_all[c_me] = total_of(c_z)
        start(C_BACK, core_group, c_all)
        sent(C_Z, z_group, c_z)
        arrived(C_BACK, core_group, c_all)
        target = c_all[...].reshape(RANK, LANES)
        times[...] = jnp.maximum(moved + scale * target, 0.0)
        sent(C_BACK, core_group, c_all)
        return carry

    lax.fori_loop(0, SWEEPS, sweep, 0)
    pick = (
        lax.broadcasted_iota(jnp.int32, (nb, LANES), 1)
        == lax.broadcasted_iota(jnp.int32, (nb, LANES), 0) + RANK
    ).astype(F32)
    bands_out[...] = dot_nt(pick, bands[...])


def body(nx, ny, nz, series, pixel_factor, band_factor, time_factor):
    nb = series.shape[0]
    vmem = pl.BlockSpec(memory_space=pltpu.VMEM)
    wide = (RANK, LANES)
    half = (HALF, LANES)

    def f32(*shape):
        return pltpu.VMEM(shape, F32)

    pixels, bands, times = pl.pallas_call(
        functools.partial(kernel, nx, ny, nz),
        out_shape=(
            jax.ShapeDtypeStruct(pixel_factor.shape, F32),
            jax.ShapeDtypeStruct(band_factor.shape, F32),
            jax.ShapeDtypeStruct(wide, F32),
        ),
        in_specs=[pl.BlockSpec(memory_space=pltpu.HBM)] + [vmem] * 3,
        out_specs=(vmem,) * 3,
        scratch_shapes=[
            pltpu.VMEM(series.shape, series.dtype),
            f32(*wide),
            f32(*wide),
            f32(nb, *wide),
            f32(nb, *pixel_factor.shape),
            f32(nb, *wide),
            f32(nx, *pixel_factor.shape),
            f32(nx, *wide),
            f32(nx, *wide),
            f32(*half),
            f32(*half),
            f32(ny, *half),
            f32(nz, *half),
            f32(2, *half),
            f32(*half),
            f32(*half),
            f32(ny, *half),
            f32(nx, *half),
            f32(nz, *half),
            f32(2, *half),
            pltpu.SemaphoreType.DMA((PHASES, 8)),
            pltpu.SemaphoreType.DMA((PHASES, 8)),
            pltpu.SemaphoreType.DMA,
        ],
        compiler_params=pltpu.CompilerParams(collective_id=0, has_side_effects=True),
    )(series, pixel_factor, band_factor, time_factor.T)
    return pixels, bands, times.T


def build(mesh, ny):
    placed = (P("band", None, "pix"), P(None, "pix"), P("band", None), P())
    return jax.shard_map(
        functools.partial(body, mesh.shape["band"], ny, mesh.shape["pix"] // (2 * ny)),
        mesh=mesh,
        in_specs=placed,
        out_specs=(P(None, "pix"), P("band", None), P()),
        check_vma=False,
    )


def solution(mesh):
    return build(mesh, 4)
```

```python
import functools

import jax
import jax.numpy as jnp
from jax import lax
from jax.experimental import pallas as pl
from jax.experimental.pallas import tpu as pltpu
from jax.sharding import PartitionSpec as P

SWEEPS = 4
RANK = 64
LANES = 128
UNROLL = 8
LONG = 56
F32 = jnp.float32
HIGH = lax.Precision.HIGHEST
MESH = pl.DeviceIdType.MESH

(
    AT_OTHER, AT_MINE, AT_GRAM, AT_FIRST, B_PAIR, B_Y, B_Z, B_BACK,
    C_PAIR, C_Y, C_X, C_Z, C_BACK, PHASES,
) = range(14)
HALF = RANK // 2


def dot_nn(a, b):
    return lax.dot_general(
        a, b, (((1,), (0,)), ((), ())), precision=HIGH, preferred_element_type=F32
    )


def dot_nt(a, b):
    return lax.dot_general(
        a, b, (((1,), (1,)), ((), ())), precision=HIGH, preferred_element_type=F32
    )


def padded_gram(a):
    return dot_nt(a, jnp.concatenate([a, jnp.zeros_like(a)], axis=0))


def step_of(gram):
    sums = jnp.sum(gram, axis=0, keepdims=True)
    return 1.0 / (jnp.max(sums, axis=1, keepdims=True) + 1e-06)


def total_of(slots):
    total = slots[0]
    for j in range(1, slots.shape[0]):
        total = total + slots[j]
    return total


def kernel(
    nx, ny, nz,
    series_in, pixels_in, bands_in, times_in,
    pixels, bands_out, times,
    series, bands, gram_b, wide, folded, spread,
    a_slots, g_slots, first_slots,
    b_send, b_pair, b_y, b_z, b_all,
    c_send, c_pair, c_y, c_x, c_z, c_all,
    send_sems, recv_sems, load_sem,
):
    nb = series.shape[0]
    load = pltpu.make_async_copy(series_in, series, load_sem)
    load.start()
    pix_me = lax.axis_index("pix")
    x_me = lax.axis_index("band")
    z_me = pix_me // (2 * ny)
    y_me = lax.rem(pix_me // 2, ny)
    c_me = lax.rem(pix_me, 2)

    def on_x(k):
        return (pix_me, k)

    def on_z(k):
        return (k * (2 * ny) + y_me * 2 + c_me, x_me)

    def on_y(k):
        return (z_me * (2 * ny) + k * 2 + c_me, x_me)

    def on_core(k):
        return (z_me * (2 * ny) + y_me * 2 + k, x_me)

    groups = ((on_x, x_me, nx), (on_z, z_me, nz), (on_y, y_me, ny), (on_core, c_me, 2))
    x_group, z_group, y_group, core_group = groups
    barrier = pltpu.get_barrier_semaphore()
    for at, me, n in groups:
        for d in range(1, n):
            pl.semaphore_signal(
                barrier, inc=1, device_id=at(lax.rem(me + d, n)), device_id_type=MESH
            )
    pl.semaphore_wait(barrier, sum(n - 1 for _, _, n in groups))

    def copies_of(phase, group, source, slots, sent):
        at, me, n = group
        copies = []
        for d in sorted(range(1, n), key=lambda d: -min(d, n - d)):
            to = lax.rem(me + d, n)
            slot = me if sent else lax.rem(me + n - d, n)
            copies.append(
                pltpu.make_async_remote_copy(
                    src_ref=slots.at[me] if source is None else source,
                    dst_ref=slots if source is not None else slots.at[slot],
                    send_sem=send_sems.at[phase, d],
                    recv_sem=recv_sems.at[phase, d],
                    device_id=at(to),
                    device_id_type=MESH,
                )
            )
        return copies

    def start(phase, group, slots, source=None):
        for copy in copies_of(phase, group, source, slots, True):
            copy.start()

    def arrived(phase, group, slots, source=None):
        for copy in copies_of(phase, group, source, slots, False):
            copy.wait_recv()

    def sent(phase, group, slots, source=None):
        for copy in copies_of(phase, group, source, slots, True):
            copy.wait_send()

    lane = lax.broadcasted_iota(jnp.int32, (RANK, LANES), 1)
    half_lane = lax.broadcasted_iota(jnp.int32, (HALF, LANES), 1)
    mine = pl.multiple_of(c_me * HALF, HALF)
    other = pl.multiple_of((1 - c_me) * HALF, HALF)

    def column(value, b):
        one = value[:, RANK + b : RANK + b + 1]
        return jnp.broadcast_to(one, (value.shape[0], LANES))

    rest = LANES - RANK - nb
    tall = [jnp.zeros((RANK, RANK), F32), bands_in[...]]
    if rest:
        tall.append(jnp.zeros((rest, RANK), F32))
    unit = (
        lax.broadcasted_iota(jnp.int32, (RANK, RANK), 0)
        == lax.broadcasted_iota(jnp.int32, (RANK, RANK), 1)
    ).astype(F32)
    first = dot_nt(unit, jnp.concatenate(tall, axis=0))
    bands[...] = first
    first_slots[x_me] = padded_gram(first)
    start(AT_FIRST, x_group, first_slots)
    pixels[...] = pixels_in[...]
    times[...] = times_in[...]
    for b in range(nb):
        wide[b] = column(first, b)
    load.wait()

    def sweep(number, carry):
        ct = times[...]
        c_low = ct.astype(jnp.bfloat16)

        def fold(i, acc):
            for u in range(LONG):
                b = i * LONG + u
                one = jnp.dot(c_low, series[b], preferred_element_type=F32)
                folded[b] = one
                weight = wide[b]
                acc = acc + one * jnp.concatenate([weight, weight], axis=1)
            return acc

        acc = lax.fori_loop(0, nb // LONG, fold, jnp.zeros(pixels.shape, F32))
        a_slots[x_me] = acc
        start(AT_OTHER, x_group, a_slots.at[:, pl.ds(other, HALF), :])
        start(AT_MINE, x_group, a_slots.at[:, pl.ds(mine, HALF), :])

        @pl.when(number == 0)
        def _():
            arrived(AT_FIRST, x_group, first_slots)
            sent(AT_FIRST, x_group, first_slots)
            gram_b[...] = total_of(first_slots)

        gram_c = dot_nt(ct, ct)
        gram = gram_b[...][:, :RANK] * gram_c
        scale = step_of(gram)
        p = pixels[...]
        pixels[...] = p - scale * dot_nn(gram, p)

        def new_rows(phase, low):
            rows = pl.ds(low, HALF)
            slots = a_slots.at[:, rows, :]
            arrived(phase, x_group, slots)
            p_rows = jnp.maximum(pixels[rows, :] + scale * total_of(slots), 0.0)
            pixels[rows, :] = p_rows
            return p_rows

        def band_part(low, p_rows):
            rows = pl.ds(low, HALF)

            def into_bands(i, acc):
                for u in range(LONG):
                    b = i * LONG + u
                    both = folded[b, rows, :] * p_rows
                    both = both[:, :LANES] + both[:, LANES:]
                    acc = jnp.where(
                        half_lane == RANK + b,
                        jnp.sum(both, axis=1, keepdims=True), acc,
                    )
                return acc

            return lax.fori_loop(0, nb // LONG, into_bands, jnp.zeros((HALF, LANES), F32))

        def spread_over(low, high):
            def some(i, carry):
                for u in range(UNROLL):
                    b = i * UNROLL + u
                    spread[b] = lax.dot_general(
                        p_low, series[b], (((1,), (1,)), ((), ())),
                        preferred_element_type=F32,
                    )
                return carry

            lax.fori_loop(low, high, some, 0)

        blocks = nb // UNROLL
        cuts = (0, (blocks + 6) // 7, (blocks * 4 + 6) // 7, blocks)
        p_other = new_rows(AT_OTHER, other)
        part = band_part(other, p_other)
        p_mine = new_rows(AT_MINE, mine)
        p = pixels[...]
        p_low = p.astype(jnp.bfloat16)
        p_tall = jnp.concatenate([p, jnp.zeros_like(p)], axis=0)
        b_send[...] = part + dot_nt(p_other, p_tall)
        start(B_PAIR, core_group, b_pair, b_send)
        own = band_part(mine, p_mine) + dot_nt(p_mine, p_tall)
        sent(AT_OTHER, x_group, a_slots.at[:, pl.ds(other, HALF), :])
        sent(AT_MINE, x_group, a_slots.at[:, pl.ds(mine, HALF), :])
        spread_over(cuts[0], cuts[1])
        arrived(B_PAIR, core_group, b_pair, b_send)
        b_y[y_me] = own + b_pair[...]
        start(B_Y, y_group, b_y)
        sent(B_PAIR, core_group, b_pair, b_send)
        spread_over(cuts[1], cuts[2])
        arrived(B_Y, y_group, b_y)
        b_z[z_me] = total_of(b_y)
        start(B_Z, z_group, b_z)
        sent(B_Y, y_group, b_y)
        spread_over(cuts[2], cuts[3])
        arrived(B_Z, z_group, b_z)
        b_all[c_me] = total_of(b_z)
        start(B_BACK, core_group, b_all)
        sent(B_Z, z_group, b_z)
        arrived(B_BACK, core_group, b_all)
        both = b_all[...].reshape(RANK, LANES)
        gram_a = both[:, :RANK]
        target = jnp.where(lane >= RANK, both, 0.0)
        gram = gram_a * gram_c
        bt = bands[...]
        bt = jnp.maximum(bt - step_of(gram) * (dot_nn(gram, bt) - target), 0.0)
        bands[...] = bt

        def time_part(low):
            rows = pl.ds(low, HALF)
            bt_rows = bands[rows, :]
            acc = jnp.zeros((HALF, LANES), F32)
            for b in range(nb):
                weight = column(bt_rows, b)
                wide[b, rows, :] = weight
                weight = weight.astype(jnp.bfloat16).astype(F32)
                acc = acc + spread[b, rows, :] * weight
            return acc

        c_send[...] = time_part(other)
        start(C_PAIR, core_group, c_pair, c_send)
        sent(B_BACK, core_group, b_all)
        g_slots[x_me] = padded_gram(bt)
        start(AT_GRAM, x_group, g_slots)
        own = time_part(mine)
        arrived(C_PAIR, core_group, c_pair, c_send)
        c_y[y_me] = own + c_pair[...]
        start(C_Y, y_group, c_y)
        sent(C_PAIR, core_group, c_pair, c_send)
        arrived(C_Y, y_group, c_y)
        c_x[x_me] = total_of(c_y)
        start(C_X, x_group, c_x)
        sent(C_Y, y_group, c_y)
        arrived(C_X, x_group, c_x)
        c_z[z_me] = total_of(c_x)
        start(C_Z, z_group, c_z)
        sent(C_X, x_group, c_x)
        arrived(AT_GRAM, x_group, g_slots)
        sent(AT_GRAM, x_group, g_slots)
        new_gram = total_of(g_slots)
        gram_b[...] = new_gram
        gram = gram_a * new_gram[:, :RANK]
        scale = step_of(gram)
        moved = ct - scale * dot_nn(gram, ct)
        arrived(C_Z, z_group, c_z)
        c_all[c_me] = total_of(c_z)
        start(C_BACK, core_group, c_all)
        sent(C_Z, z_group, c_z)
        arrived(C_BACK, core_group, c_all)
        target = c_all[...].reshape(RANK, LANES)
        times[...] = jnp.maximum(moved + scale * target, 0.0)
        sent(C_BACK, core_group, c_all)
        return carry

    lax.fori_loop(0, SWEEPS, sweep, 0)
    pick = (
        lax.broadcasted_iota(jnp.int32, (nb, LANES), 1)
        == lax.broadcasted_iota(jnp.int32, (nb, LANES), 0) + RANK
    ).astype(F32)
    bands_out[...] = dot_nt(pick, bands[...])


def body(nx, ny, nz, series, pixel_factor, band_factor, time_factor):
    nb = series.shape[0]
    vmem = pl.BlockSpec(memory_space=pltpu.VMEM)
    wide = (RANK, LANES)
    half = (HALF, LANES)

    def f32(*shape):
        return pltpu.VMEM(shape, F32)

    pixels, bands, times = pl.pallas_call(
        functools.partial(kernel, nx, ny, nz),
        out_shape=(
            jax.ShapeDtypeStruct(pixel_factor.shape, F32),
            jax.ShapeDtypeStruct(band_factor.shape, F32),
            jax.ShapeDtypeStruct(wide, F32),
        ),
        in_specs=[pl.BlockSpec(memory_space=pltpu.HBM)] + [vmem] * 3,
        out_specs=(vmem,) * 3,
        scratch_shapes=[
            pltpu.VMEM(series.shape, series.dtype),
            f32(*wide),
            f32(*wide),
            f32(nb, *wide),
            f32(nb, *pixel_factor.shape),
            f32(nb, *wide),
            f32(nx, *pixel_factor.shape),
            f32(nx, *wide),
            f32(nx, *wide),
            f32(*half),
            f32(*half),
            f32(ny, *half),
            f32(nz, *half),
            f32(2, *half),
            f32(*half),
            f32(*half),
            f32(ny, *half),
            f32(nx, *half),
            f32(nz, *half),
            f32(2, *half),
            pltpu.SemaphoreType.DMA((PHASES, 8)),
            pltpu.SemaphoreType.DMA((PHASES, 8)),
            pltpu.SemaphoreType.DMA,
        ],
        compiler_params=pltpu.CompilerParams(collective_id=0, has_side_effects=True),
    )(series, pixel_factor, band_factor, time_factor.T)
    return pixels, bands, times.T


def build(mesh, ny):
    placed = (P("band", None, "pix"), P(None, "pix"), P("band", None), P())
    return jax.shard_map(
        functools.partial(body, mesh.shape["band"], ny, mesh.shape["pix"] // (2 * ny)),
        mesh=mesh,
        in_specs=placed,
        out_specs=(P(None, "pix"), P("band", None), P()),
        check_vma=False,
    )


def solution(mesh):
    return build(mesh, 4)
```

```python
import functools

import jax
import jax.numpy as jnp
from jax import lax
from jax.experimental import pallas as pl
from jax.experimental.pallas import tpu as pltpu
from jax.sharding import PartitionSpec as P

SWEEPS = 4
RANK = 64
LANES = 128
UNROLL = 8
LONG = 56
F32 = jnp.float32
HIGH = lax.Precision.HIGHEST
MESH = pl.DeviceIdType.MESH

(
    AT_OTHER, AT_MINE, AT_GRAM, AT_FIRST, B_PAIR, B_Y, B_Z, B_BACK,
    C_PAIR, C_Y, C_X, C_Z, C_BACK, PHASES,
) = range(14)
HALF = RANK // 2


def dot_nn(a, b):
    return lax.dot_general(
        a, b, (((1,), (0,)), ((), ())), precision=HIGH, preferred_element_type=F32
    )


def dot_nt(a, b):
    return lax.dot_general(
        a, b, (((1,), (1,)), ((), ())), precision=HIGH, preferred_element_type=F32
    )


def padded_gram(a):
    return dot_nt(a, jnp.concatenate([a, jnp.zeros_like(a)], axis=0))


def step_of(gram):
    sums = jnp.sum(gram, axis=0, keepdims=True)
    return 1.0 / (jnp.max(sums, axis=1, keepdims=True) + 1e-06)


def total_of(slots):
    total = slots[0]
    for j in range(1, slots.shape[0]):
        total = total + slots[j]
    return total


def kernel(
    nx, ny, nz,
    series_in, pixels_in, bands_in, times_in,
    pixels, bands_out, times,
    series, bands, gram_b, wide, folded, spread,
    a_slots, g_slots, first_slots,
    b_send, b_pair, b_y, b_z, b_all,
    c_send, c_pair, c_y, c_x, c_z, c_all,
    send_sems, recv_sems, load_sem,
):
    nb = series.shape[0]
    load = pltpu.make_async_copy(series_in, series, load_sem)
    load.start()
    pix_me = lax.axis_index("pix")
    x_me = lax.axis_index("band")
    z_me = pix_me // (2 * ny)
    y_me = lax.rem(pix_me // 2, ny)
    c_me = lax.rem(pix_me, 2)

    def on_x(k):
        return (pix_me, k)

    def on_z(k):
        return (k * (2 * ny) + y_me * 2 + c_me, x_me)

    def on_y(k):
        return (z_me * (2 * ny) + k * 2 + c_me, x_me)

    def on_core(k):
        return (z_me * (2 * ny) + y_me * 2 + k, x_me)

    groups = ((on_x, x_me, nx), (on_z, z_me, nz), (on_y, y_me, ny), (on_core, c_me, 2))
    x_group, z_group, y_group, core_group = groups
    barrier = pltpu.get_barrier_semaphore()
    for at, me, n in groups:
        for d in range(1, n):
            pl.semaphore_signal(
                barrier, inc=1, device_id=at(lax.rem(me + d, n)), device_id_type=MESH
            )
    pl.semaphore_wait(barrier, sum(n - 1 for _, _, n in groups))

    def copies_of(phase, group, source, slots, sent):
        at, me, n = group
        copies = []
        for d in sorted(range(1, n), key=lambda d: -min(d, n - d)):
            to = lax.rem(me + d, n)
            slot = me if sent else lax.rem(me + n - d, n)
            copies.append(
                pltpu.make_async_remote_copy(
                    src_ref=slots.at[me] if source is None else source,
                    dst_ref=slots if source is not None else slots.at[slot],
                    send_sem=send_sems.at[phase, d],
                    recv_sem=recv_sems.at[phase, d],
                    device_id=at(to),
                    device_id_type=MESH,
                )
            )
        return copies

    def start(phase, group, slots, source=None):
        for copy in copies_of(phase, group, source, slots, True):
            copy.start()

    def arrived(phase, group, slots, source=None):
        for copy in copies_of(phase, group, source, slots, False):
            copy.wait_recv()

    def sent(phase, group, slots, source=None):
        for copy in copies_of(phase, group, source, slots, True):
            copy.wait_send()

    lane = lax.broadcasted_iota(jnp.int32, (RANK, LANES), 1)
    half_lane = lax.broadcasted_iota(jnp.int32, (HALF, LANES), 1)
    mine = pl.multiple_of(c_me * HALF, HALF)
    other = pl.multiple_of((1 - c_me) * HALF, HALF)

    def column(value, b):
        one = value[:, RANK + b : RANK + b + 1]
        return jnp.broadcast_to(one, (value.shape[0], LANES))

    rest = LANES - RANK - nb
    tall = [jnp.zeros((RANK, RANK), F32), bands_in[...]]
    if rest:
        tall.append(jnp.zeros((rest, RANK), F32))
    unit = (
        lax.broadcasted_iota(jnp.int32, (RANK, RANK), 0)
        == lax.broadcasted_iota(jnp.int32, (RANK, RANK), 1)
    ).astype(F32)
    first = dot_nt(unit, jnp.concatenate(tall, axis=0))
    bands[...] = first
    first_slots[x_me] = padded_gram(first)
    start(AT_FIRST, x_group, first_slots)
    pixels[...] = pixels_in[...]
    times[...] = times_in[...]
    for b in range(nb):
        wide[b] = column(first, b)
    load.wait()

    def sweep(number, carry):
        ct = times[...]
        c_low = ct.astype(jnp.bfloat16)

        def fold(i, acc):
            for u in range(LONG):
                b = i * LONG + u
                one = jnp.dot(c_low, series[b], preferred_element_type=F32)
                folded[b] = one
                weight = wide[b]
                acc = acc + one * jnp.concatenate([weight, weight], axis=1)
            return acc

        acc = lax.fori_loop(0, nb // LONG, fold, jnp.zeros(pixels.shape, F32))
        a_slots[x_me] = acc
        start(AT_OTHER, x_group, a_slots.at[:, pl.ds(other, HALF), :])
        start(AT_MINE, x_group, a_slots.at[:, pl.ds(mine, HALF), :])

        @pl.when(number == 0)
        def _():
            arrived(AT_FIRST, x_group, first_slots)
            sent(AT_FIRST, x_group, first_slots)
            gram_b[...] = total_of(first_slots)

        gram_c = dot_nt(ct, ct)
        gram = gram_b[...][:, :RANK] * gram_c
        scale = step_of(gram)
        p = pixels[...]
        pixels[...] = p - scale * dot_nn(gram, p)

        def new_rows(phase, low):
            rows = pl.ds(low, HALF)
            slots = a_slots.at[:, rows, :]
            arrived(phase, x_group, slots)
            p_rows = jnp.maximum(pixels[rows, :] + scale * total_of(slots), 0.0)
            pixels[rows, :] = p_rows
            return p_rows

        def band_part(low, p_rows):
            rows = pl.ds(low, HALF)

            def into_bands(i, acc):
                for u in range(LONG):
                    b = i * LONG + u
                    both = folded[b, rows, :] * p_rows
                    both = both[:, :LANES] + both[:, LANES:]
                    acc = jnp.where(
                        half_lane == RANK + b,
                        jnp.sum(both, axis=1, keepdims=True), acc,
                    )
                return acc

            return lax.fori_loop(0, nb // LONG, into_bands, jnp.zeros((HALF, LANES), F32))

        def spread_over(low, high):
            def some(i, carry):
                for u in range(UNROLL):
                    b = i * UNROLL + u
                    spread[b] = lax.dot_general(
                        p_low, series[b], (((1,), (1,)), ((), ())),
                        preferred_element_type=F32,
                    )
                return carry

            lax.fori_loop(low, high, some, 0)

        blocks = nb // UNROLL
        cut = (blocks * 4 + 6) // 7
        p_other = new_rows(AT_OTHER, other)
        part = band_part(other, p_other)
        p_mine = new_rows(AT_MINE, mine)
        p = pixels[...]
        p_low = p.astype(jnp.bfloat16)
        p_tall = jnp.concatenate([p, jnp.zeros_like(p)], axis=0)
        b_send[...] = part + dot_nt(p_other, p_tall)
        start(B_PAIR, core_group, b_pair, b_send)
        own = band_part(mine, p_mine) + dot_nt(p_mine, p_tall)
        sent(AT_OTHER, x_group, a_slots.at[:, pl.ds(other, HALF), :])
        sent(AT_MINE, x_group, a_slots.at[:, pl.ds(mine, HALF), :])
        arrived(B_PAIR, core_group, b_pair, b_send)
        b_y[y_me] = own + b_pair[...]
        start(B_Y, y_group, b_y)
        sent(B_PAIR, core_group, b_pair, b_send)
        spread_over(0, cut)
        arrived(B_Y, y_group, b_y)
        b_z[z_me] = total_of(b_y)
        start(B_Z, z_group, b_z)
        sent(B_Y, y_group, b_y)
        spread_over(cut, blocks)
        arrived(B_Z, z_group, b_z)
        b_all[c_me] = total_of(b_z)
        start(B_BACK, core_group, b_all)
        sent(B_Z, z_group, b_z)
        arrived(B_BACK, core_group, b_all)
        both = b_all[...].reshape(RANK, LANES)
        gram_a = both[:, :RANK]
        target = jnp.where(lane >= RANK, both, 0.0)
        gram = gram_a * gram_c
        bt = bands[...]
        bt = jnp.maximum(bt - step_of(gram) * (dot_nn(gram, bt) - target), 0.0)
        bands[...] = bt

        def time_part(low):
            rows = pl.ds(low, HALF)
            bt_rows = bands[rows, :]
            acc = jnp.zeros((HALF, LANES), F32)
            for b in range(nb):
                weight = column(bt_rows, b)
                wide[b, rows, :] = weight
                weight = weight.astype(jnp.bfloat16).astype(F32)
                acc = acc + spread[b, rows, :] * weight
            return acc

        c_send[...] = time_part(other)
        start(C_PAIR, core_group, c_pair, c_send)
        sent(B_BACK, core_group, b_all)
        g_slots[x_me] = padded_gram(bt)
        start(AT_GRAM, x_group, g_slots)
        own = time_part(mine)
        arrived(C_PAIR, core_group, c_pair, c_send)
        c_y[y_me] = own + c_pair[...]
        start(C_Y, y_group, c_y)
        sent(C_PAIR, core_group, c_pair, c_send)
        arrived(C_Y, y_group, c_y)
        c_x[x_me] = total_of(c_y)
        start(C_X, x_group, c_x)
        sent(C_Y, y_group, c_y)
        arrived(C_X, x_group, c_x)
        c_z[z_me] = total_of(c_x)
        start(C_Z, z_group, c_z)
        sent(C_X, x_group, c_x)
        arrived(AT_GRAM, x_group, g_slots)
        sent(AT_GRAM, x_group, g_slots)
        new_gram = total_of(g_slots)
        gram_b[...] = new_gram
        gram = gram_a * new_gram[:, :RANK]
        scale = step_of(gram)
        moved = ct - scale * dot_nn(gram, ct)
        arrived(C_Z, z_group, c_z)
        c_all[c_me] = total_of(c_z)
        start(C_BACK, core_group, c_all)
        sent(C_Z, z_group, c_z)
        arrived(C_BACK, core_group, c_all)
        target = c_all[...].reshape(RANK, LANES)
        times[...] = jnp.maximum(moved + scale * target, 0.0)
        sent(C_BACK, core_group, c_all)
        return carry

    lax.fori_loop(0, SWEEPS, sweep, 0)
    pick = (
        lax.broadcasted_iota(jnp.int32, (nb, LANES), 1)
        == lax.broadcasted_iota(jnp.int32, (nb, LANES), 0) + RANK
    ).astype(F32)
    bands_out[...] = dot_nt(pick, bands[...])


def body(nx, ny, nz, series, pixel_factor, band_factor, time_factor):
    nb = series.shape[0]
    vmem = pl.BlockSpec(memory_space=pltpu.VMEM)
    wide = (RANK, LANES)
    half = (HALF, LANES)

    def f32(*shape):
        return pltpu.VMEM(shape, F32)

    pixels, bands, times = pl.pallas_call(
        functools.partial(kernel, nx, ny, nz),
        out_shape=(
            jax.ShapeDtypeStruct(pixel_factor.shape, F32),
            jax.ShapeDtypeStruct(band_factor.shape, F32),
            jax.ShapeDtypeStruct(wide, F32),
        ),
        in_specs=[pl.BlockSpec(memory_space=pltpu.HBM)] + [vmem] * 3,
        out_specs=(vmem,) * 3,
        scratch_shapes=[
            pltpu.VMEM(series.shape, series.dtype),
            f32(*wide),
            f32(*wide),
            f32(nb, *wide),
            f32(nb, *pixel_factor.shape),
            f32(nb, *wide),
            f32(nx, *pixel_factor.shape),
            f32(nx, *wide),
            f32(nx, *wide),
            f32(*half),
            f32(*half),
            f32(ny, *half),
            f32(nz, *half),
            f32(2, *half),
            f32(*half),
            f32(*half),
            f32(ny, *half),
            f32(nx, *half),
            f32(nz, *half),
            f32(2, *half),
            pltpu.SemaphoreType.DMA((PHASES, 8)),
            pltpu.SemaphoreType.DMA((PHASES, 8)),
            pltpu.SemaphoreType.DMA,
        ],
        compiler_params=pltpu.CompilerParams(collective_id=0, has_side_effects=True),
    )(series, pixel_factor, band_factor, time_factor.T)
    return pixels, bands, times.T


def build(mesh, ny):
    placed = (P("band", None, "pix"), P(None, "pix"), P("band", None), P())
    return jax.shard_map(
        functools.partial(body, mesh.shape["band"], ny, mesh.shape["pix"] // (2 * ny)),
        mesh=mesh,
        in_specs=placed,
        out_specs=(P(None, "pix"), P("band", None), P()),
        check_vma=False,
    )


def solution(mesh):
    return build(mesh, 4)
```
